32 devices in a mesh: grp: 4 (over y, x), tp: 4 (over z), seq: 2 (over core).
Axes of the slice: x: 2, y: 2, z: 4, core: 2. Of those that a mesh axis runs over, the one named last changes fastest.
Arguments:
- grads: bfloat16 [8, 4096, 8192], P(('grp', 'seq'), 'tp'), may hold values from -6 to 6
- master: float32 [4096, 8192], P('tp', 'grp'), may hold values from -0.09375 to 0.09375
- moment: float32 [4096, 8192], P('tp', 'grp'), may hold values from -3 to 3
- second: float32 [4096, 8192], P('tp', 'grp'), may hold values from 0.0001 to 1
- queries: bfloat16 [4096, 4096], P(('grp', 'seq'), 'tp'), may hold values from -7 to 7
- keys: bfloat16 [4096, 512], P(('grp', 'seq')), may hold values from -6 to 6
- values: bfloat16 [4096, 512], P(('grp', 'seq')), may hold values from -6 to 6
- resid: bfloat16 [4096, 8192], P(('grp', 'seq'), 'tp'), may hold values from -6 to 6
- segs: int32 [4096], replicated, may hold values from 0 to 15, never falling along the last dimension, each value on 1 to 512 neighbouring positions
Outputs:
- master_new: float32 [4096, 8192], P('tp', 'grp')
- moment_new: float32 [4096, 8192], P('tp', 'grp')
- second_new: float32 [4096, 8192], P('tp', 'grp')
- layer_out: bfloat16 [4096, 8192], P(('grp', 'seq'), 'tp')
The draws below stay inside these ranges and needn't reach their ends.
Inputs may be any that keep to these rules, and one draw needn't show every extreme that they name: `segs`: numbered from 0 in order of position and never falling; each trajectory is a run of 1 to 512 positions.
All inputs are finite; a program needn't handle non-finite values.
Results may differ from the reference program's by a relative error of at most 0.0085.
Values may be sent and summed in bfloat16 or wider, within the bound.
A program may use at most 192 MiB of HBM per device.

```python
import math
import jax
import jax.numpy as jnp
import numpy as np
from jax import lax

D = 8192
HD = 128
HQ = 32
KVH = 4
TOK_DEV = 512
TOKENS = 4096
REPL = 8
N_GRP = 4
N_SEQ = 2


def paired_draw(key):
    base = jax.random.fold_in(key, 7301)
    query_key, key_key = jax.random.split(base, 2)
    query_all = jnp.clip(jax.random.normal(query_key, (TOKENS, HQ, HD), jnp.float32), -6.0, 6.0)
    key_all = jnp.clip(jax.random.normal(key_key, (TOKENS, KVH, HD), jnp.float32), -6.0, 6.0)
    return (query_all.reshape(TOKENS, HQ * HD), key_all.reshape(TOKENS, KVH * HD))


def draw_queries(key, part):
    return paired_draw(key)[0].astype(jnp.bfloat16)


def draw_keys(key, part):
    return paired_draw(key)[1].astype(jnp.bfloat16)


def with_spikes(result, own_key, source, target, parts, factor):
    def block_of(dim):
        return (jnp.arange(result.shape[dim]) // (result.shape[dim] // parts)).reshape((-1,) + (1,) * (result.ndim - 1 - dim))

    first = jax.random.permutation(own_key, parts)[block_of(target)]
    other_side = (block_of(target) + parts // 2) % parts
    return jnp.where((block_of(source) == first) | (block_of(source) == other_side), factor * result, result)


def shard_levels(own_key, dims, cuts, least, high):
    def one(dim, shards_of):
        steps = jax.random.uniform(jax.random.fold_in(jax.random.fold_in(own_key, 6), dim), (shards_of,), jnp.float32, least / len(cuts), high / len(cuts))
        return jnp.repeat(jnp.exp(steps), dims[dim] // shards_of).reshape((-1,) + (1,) * (len(dims) - dim - 1))

    gain = one(*cuts[0])
    for cut in cuts[1:]:
        gain = gain * one(*cut)
    return gain


def length_profile(amount, total, reach, skew):
    weights = [(1 << 20) // math.isqrt(grade ** skew) + 1 for grade in range(2, amount + 1)]
    spare, given = total - reach - (amount - 1), [1] * (amount - 1)
    while spare > 0:
        free = [i for i in range(amount - 1) if given[i] < reach]
        mass, remaining = sum([weights[i] for i in free]), spare
        for i in free:
            more = min(reach - given[i], max(1, remaining * weights[i] // mass), spare)
            given[i] = given[i] + more
            spare = spare - more
    return np.array([reach] + given)


def ragged_sizes(stream_key, amount, total, reach, slope):
    if amount == 2:
        one = jax.random.randint(stream_key, (), max(1, total - reach), min(reach, total - 1) + 1)
        return jnp.stack([one, total - one])
    tallies = jnp.asarray(length_profile(amount, total, reach, slope), jnp.int32)
    pairs = (amount - 1) // 2
    donor, sink = tallies[1:1 + 2 * pairs:2], tallies[2:2 + 2 * pairs:2]
    room = jnp.minimum(donor - 1, reach - sink)
    passed = jax.random.randint(jax.random.fold_in(stream_key, 1), (pairs,), 0, 1 << 20) % (room + 1)
    tallies = tallies.at[1:1 + 2 * pairs:2].set(donor - passed).at[2:2 + 2 * pairs:2].set(sink + passed)
    return tallies[jax.random.permutation(jax.random.fold_in(stream_key, 2), amount)]


def bell_draw(key, shape, scale, bound, pieces=(), held_as=jnp.bfloat16):
    entries = scale * jax.random.normal(key, shape, jnp.float32)
    if pieces:
        entries = entries * shard_levels(key, shape, pieces, -0.22, 0.18)
    return jnp.clip(entries, -bound, bound).astype(held_as)


def bell_draw_with(own_key, dims, scale, bound, shards, heavy, kind=jnp.bfloat16):
    entries = scale * jax.random.normal(own_key, dims, jnp.float32)
    if shards:
        entries = entries * shard_levels(own_key, dims, shards, -0.22, 0.18)
    return jnp.clip(with_spikes(entries, jax.random.fold_in(own_key, 3), *heavy), -bound, bound).astype(kind)


def setup_inputs(seed: int = 0) -> dict:
    splits = jax.random.split(jax.random.key(seed), 10)
    grads = bell_draw_with(splits[0], (REPL, HQ * HD, D), 1.0, 6.0, ((0, 8), (1, 4)), (0, 2, 8, 2.0))
    master = bell_draw(splits[1], (HQ * HD, D), (HQ * HD) ** -0.5, 0.09375, ((0, 4), (1, 4)), jnp.float32)
    moment = bell_draw(splits[2], (HQ * HD, D), 0.2, 3.0, ((0, 4), (1, 4)), jnp.float32)
    second = jnp.clip(jnp.exp(math.log(1.0) - 9.2103404 * jax.random.uniform(splits[3], (HQ * HD, D), jnp.float32) ** shard_levels(splits[3], (HQ * HD, D), ((0, 4), (1, 4)), -0.2, 0.2)), 0.0001, 1.0)
    queries = draw_queries(jax.random.fold_in(splits[9], 71), 0)
    keys = draw_keys(jax.random.fold_in(splits[9], 71), 0)
    values = bell_draw(splits[6], (TOKENS, KVH * HD), 1.0, 6.0, ((0, 8),))
    resid = bell_draw(splits[7], (TOKENS, D), 1.0, 6.0, ((0, 8), (1, 4)))
    segs = jnp.searchsorted(jnp.cumsum(ragged_sizes(splits[8], 2 * N_GRP * N_SEQ, TOKENS, TOK_DEV, 1)), jnp.arange(TOKENS), side="right").astype(jnp.int32)
    return dict(grads=grads, master=master, moment=moment, second=second, queries=queries, keys=keys, values=values, resid=resid, segs=segs)


beta_one = 0.9
beta_two = 0.95
learn_rate = 0.001
decay_rate = 0.1
adam_eps = 1e-08

def reference(grads, master, moment, second, queries, keys, values, resid, segs):

    def accumulate(index, running):
        return running + grads[index].astype(jnp.float32)
    summed = lax.fori_loop(0, grads.shape[0], accumulate, jnp.zeros(master.shape, jnp.float32))
    gradient = summed / REPL
    moment_new = beta_one * moment + (1.0 - beta_one) * gradient
    second_new = beta_two * second + (1.0 - beta_two) * gradient * gradient
    first_hat = moment_new / (1.0 - beta_one ** 10)
    second_hat = second_new / (1.0 - beta_two ** 10)
    master_new = master - learn_rate * (first_hat / (jnp.sqrt(second_hat) + adam_eps) + decay_rate * master)
    weight = master_new.astype(jnp.bfloat16)
    position = jnp.arange(TOKENS, dtype=jnp.int32)
    visible = (position[None, :] <= position[:, None]) & (segs[None, :] == segs[:, None])
    scale = 1.0 / HD ** 0.5

    def one_head(head):
        query_rows = lax.dynamic_slice_in_dim(queries, head * HD, HD, 1)
        key_head = head // (HQ // KVH)
        key_rows = lax.dynamic_slice_in_dim(keys, key_head * HD, HD, 1)
        value_rows = lax.dynamic_slice_in_dim(values, key_head * HD, HD, 1)
        scores = jnp.dot(query_rows, key_rows.T, preferred_element_type=jnp.float32) * scale
        masked = jnp.where(visible, scores, -1e+30)
        largest = lax.optimization_barrier(jnp.max(masked, axis=1, keepdims=True))
        expo = jnp.where(visible, jnp.exp(masked - largest), 0.0)
        probs = (expo / lax.optimization_barrier(jnp.sum(expo, axis=1, keepdims=True))).astype(jnp.bfloat16)
        return jnp.dot(probs, value_rows, preferred_element_type=jnp.float32).astype(jnp.bfloat16)
    heads_out = lax.map(one_head, jnp.arange(HQ, dtype=jnp.int32))
    attn = jnp.transpose(heads_out, (1, 0, 2)).reshape(TOKENS, HQ * HD)
    layer_out = (resid.astype(jnp.float32) + jnp.dot(attn, weight, preferred_element_type=jnp.float32)).astype(jnp.bfloat16)
    return (master_new, moment_new, second_new, layer_out)
```

```python
import functools

import jax
import jax.numpy as jnp
from jax import lax
from jax.experimental import pallas as pl
from jax.experimental.pallas import tpu as pltpu
from jax.sharding import PartitionSpec as P

HD = 128
HQ = 32
KVH = 4


beta_one = 0.9
beta_two = 0.95
learn_rate = 0.001
decay_rate = 0.1
adam_eps = 1e-08


def from_behind(x, axis, by):
    count = lax.axis_size(axis)
    pairs = [(i, i + by) for i in range(count) if 0 <= i + by < count]
    return lax.ppermute(x, axis, pairs)


def body(grads, master, moment, second, queries, keys, values, resid, segs):
    partial_sum = lax.psum_scatter(grads[0], "grp", scatter_dimension=1, tiled=True).astype(
        jnp.float32
    )
    summed = lax.psum(partial_sum.astype(jnp.bfloat16), "seq").astype(jnp.float32)
    gradient = summed / (lax.axis_size("grp") * lax.axis_size("seq"))
    moment_new = beta_one * moment + (1.0 - beta_one) * gradient
    second_new = beta_two * second + (1.0 - beta_two) * gradient * gradient
    first_hat = moment_new / (1.0 - beta_one**10)
    second_hat = second_new / (1.0 - beta_two**10)
    master_new = master - learn_rate * (
        first_hat / (jnp.sqrt(second_hat) + adam_eps) + decay_rate * master
    )
    weight_block = master_new.astype(jnp.bfloat16)
    tok_rows = queries.shape[0]
    heads_here = queries.shape[1] // HD
    key_head = lax.axis_index("tp") * heads_here // (HQ // KVH)
    own_keys = lax.dynamic_slice_in_dim(keys, key_head * HD, HD, 1)
    own_values = lax.dynamic_slice_in_dim(values, key_head * HD, HD, 1)
    prior_k, prior_v = from_behind((own_keys, own_values), ("grp", "seq"), 1)
    all_keys = jnp.concatenate([prior_k, own_keys], axis=0)
    all_values = jnp.concatenate([prior_v, own_values], axis=0)
    start = lax.axis_index(("grp", "seq")) * tok_rows
    seg_here = lax.dynamic_slice_in_dim(segs, start, tok_rows, 0)
    seg_prior = lax.dynamic_slice_in_dim(segs, jnp.maximum(start - tok_rows, 0), tok_rows, 0)
    key_segs = jnp.concatenate([seg_prior, seg_here], axis=0)
    query_pos = start + jnp.arange(tok_rows, dtype=jnp.int32)
    key_pos = start - tok_rows + jnp.arange(2 * tok_rows, dtype=jnp.int32)
    visible = (
        (key_pos[None, :] >= 0)
        & (key_pos[None, :] <= query_pos[:, None])
        & (key_segs[None, :] == seg_here[:, None])
    )
    query_heads = queries.reshape(tok_rows, heads_here, HD)
    scores = jnp.einsum(
        "qhd,kd->hqk", query_heads, all_keys, preferred_element_type=jnp.float32
    ) * (1.0 / HD**0.5)
    masked = jnp.where(visible[None], scores, -1e30)
    largest = jnp.max(masked, axis=2, keepdims=True)
    expo = jnp.where(visible[None], jnp.exp(masked - largest), 0.0)
    probs = (expo / jnp.sum(expo, axis=2, keepdims=True)).astype(jnp.bfloat16)
    heads_out = jnp.einsum("hqk,kd->qhd", probs, all_values, preferred_element_type=jnp.float32)
    attn = heads_out.astype(jnp.bfloat16).reshape(tok_rows, heads_here * HD)
    partial_out = jnp.dot(
        attn,
        lax.all_gather(weight_block, "grp", axis=1, tiled=True),
        preferred_element_type=jnp.float32,
    )
    mixed = lax.psum_scatter(
        partial_out.astype(jnp.bfloat16), "tp", scatter_dimension=1, tiled=True
    ).astype(jnp.float32)
    layer_out = (resid.astype(jnp.float32) + mixed).astype(jnp.bfloat16)
    return (master_new, moment_new, second_new, layer_out)


WIDE = 128


def fused_kernel(
    grads, master, moment, second, queries, keys, values, segs,
    gsum, mixed,
    own, recv1, recv2, recv3, wg, rz, attn, qbuf, kbuf, vbuf, adam, segk,
    own_sem, pair_s, pair_r, st1_s, st1_r, st2_s, st2_r, st3_s, st3_r, st3_l,
    ag_s, ag_r, z_s, z_r, fin_s, fin_r, fin_l, adam_sem, in_sem, kv_s, kv_r, at_s, at_r,
):
    rows = master.shape[0]
    blk = master.shape[1]
    half = blk // 2
    chunks = half // WIDE
    n_grp = lax.axis_size("grp")
    n_tp = lax.axis_size("tp")
    tok = queries.shape[0]
    f32 = jnp.float32
    bf16 = jnp.bfloat16
    g = lax.axis_index("grp")
    t = lax.axis_index("tp")
    s = lax.axis_index("seq")
    x = lax.rem(g, 2)
    across_x = g + 1 - 2 * x
    across_y = g + 2 - 4 * lax.div(g, 2)
    one = across_x * (1 - s) + across_y * s
    two = across_y * (1 - s) + across_x * s
    diag = 3 - g
    up = lax.rem(t + 1, n_tp)
    down = lax.rem(t + n_tp - 1, n_tp)
    spot = 2 * g + s
    n_spot = 2 * n_grp
    after = lax.rem(spot + 1, n_spot)
    before = lax.rem(spot + n_spot - 1, n_spot)

    def dev(gg, tt, ss):
        return {"grp": gg, "tp": tt, "seq": ss}

    peer = dev(g, t, 1 - s)
    first = dev(one, t, s)
    last = dev(two, t, s)
    above = dev(g, up, s)
    below = dev(g, down, s)
    nxt = dev(lax.div(after, 2), t, lax.rem(after, 2))
    prv = dev(lax.div(before, 2), t, lax.rem(before, 2))

    def remote(src, dst, a, b, to):
        return pltpu.make_async_remote_copy(
            src_ref=src, dst_ref=dst, send_sem=a, recv_sem=b,
            device_id=to, device_id_type=pl.DeviceIdType.MESH,
        )

    def cols(start):
        return pl.ds(pl.multiple_of(start, WIDE), WIDE)

    def take(j, b):
        return pltpu.make_async_copy(
            grads.at[0, :, cols(b * blk + s * half + j * WIDE)], own.at[j, b], own_sem.at[j, b]
        )

    def pair(j, b):
        return remote(
            grads.at[0, :, cols(b * blk + (1 - s) * half + j * WIDE)],
            recv1.at[j, b], pair_s.at[j, b], pair_r.at[j, b], peer,
        )

    def state(j, k):
        ref = (master, moment, second)[k]
        slot = lax.rem(j, 3)
        return pltpu.make_async_copy(
            ref.at[:, cols(s * half + j * WIDE)], adam.at[slot, k], adam_sem.at[slot, k]
        )

    def hop_one(j, k):
        b = (one, diag)[k]
        return remote(own.at[j, b], recv2.at[j, k], st1_s.at[j, k], st1_r.at[j, k], first)

    def hop_two(j):
        return remote(own.at[j, two], recv3.at[j], st2_s.at[j], st2_r.at[j], last)

    def share(j):
        where = cols(s * half + j * WIDE)
        return remote(own.at[j, g], gsum.at[:, where], st3_s.at[j], st3_r.at[j], peer)

    def keep(j):
        where = cols(s * half + j * WIDE)
        return pltpu.make_async_copy(own.at[j, g], gsum.at[:, where], st3_l.at[j])

    def spread(j, k):
        b = (g, g, two)[k]
        to = (last, first, first)[k]
        part = wg.at[j, :, cols(b * WIDE)]
        return remote(part, part, ag_s.at[j, k], ag_r.at[j, k], to)

    def ring(j, d, r):
        b = lax.rem(t + 2 * n_tp - 1 - r, n_tp) if d == 0 else lax.rem(t + 1 + r, n_tp)
        return remote(
            recv1.at[j, b, pl.ds(d * tok, tok)], rz.at[j, d, r],
            z_s.at[j, 3 * d + r], z_r.at[j, 3 * d + r], above if d == 0 else below,
        )

    def final_peer(j):
        src = recv1.at[j, t, pl.ds(pl.multiple_of((1 - s) * tok, tok), tok)]
        return remote(src, mixed.at[:, cols(s * half + j * WIDE)], fin_s.at[j], fin_r.at[j], peer)

    def final_own(j):
        src = recv1.at[j, t, pl.ds(pl.multiple_of(s * tok, tok), tok)]
        return pltpu.make_async_copy(src, mixed.at[:, cols(s * half + j * WIDE)], fin_l.at[j])

    def fetch(j):
        for b in range(4):
            pair(j, b).start()
            take(j, b).start()

    step = 128
    q_rows = 128
    q_blocks = tok // q_rows

    def attn_part(i):
        part = attn.at[pl.ds(pl.multiple_of(s * tok + i * q_rows, q_rows), q_rows)]
        return remote(part, part, at_s.at[i], at_r.at[i], peer)

    q_copy = pltpu.make_async_copy(queries, qbuf, in_sem.at[0])
    k_copy = pltpu.make_async_copy(keys.at[:, cols(t * WIDE)], kbuf.at[pl.ds(tok, tok)], in_sem.at[1])
    v_copy = pltpu.make_async_copy(values.at[:, cols(t * WIDE)], vbuf.at[pl.ds(tok, tok)], in_sem.at[2])
    k_send = remote(keys.at[:, cols(t * WIDE)], kbuf.at[pl.ds(0, tok)], kv_s.at[0], kv_r.at[0], nxt)
    v_send = remote(values.at[:, cols(t * WIDE)], vbuf.at[pl.ds(0, tok)], kv_s.at[1], kv_r.at[1], nxt)

    barrier = pltpu.get_barrier_semaphore()
    for who in (peer, first, last, above, below, nxt, prv):
        pl.semaphore_signal(barrier, inc=1, device_id=who, device_id_type=pl.DeviceIdType.MESH)
    q_copy.start()
    k_copy.start()
    v_copy.start()
    pl.semaphore_wait(barrier, 7)
    fetch(0)
    k_send.start()
    v_send.start()
    fetch(1)
    fetch(2)
    segk[:, pl.ds(0, tok)] = segs[:, pl.ds(pl.multiple_of(before * tok, tok), tok)].astype(f32)
    segk[:, pl.ds(tok, tok)] = segs[:, pl.ds(pl.multiple_of(spot * tok, tok), tok)].astype(f32)

    def over_rows(count, size, fn):
        @pl.loop(0, count)
        def _(i):
            fn(pl.ds(pl.multiple_of(i * size, size), size))

    def stage_one(j):
        for b in range(4):
            take(j, b).wait()
            pair(j, b).wait_recv()
        for k in range(2):
            b = (one, diag)[k]

            def add(r):
                total = own[j, b, r, :].astype(f32) + recv1[j, b, r, :].astype(f32)
                own[j, b, r, :] = total.astype(bf16)

            over_rows(rows // step, step, add)
            hop_one(j, k).start()

    def stage_two(j):
        hop_one(j, 1).wait_recv()

        def add(r):
            total = own[j, two, r, :].astype(f32) + recv1[j, two, r, :].astype(f32)
            own[j, two, r, :] = (total + recv2[j, 1, r, :].astype(f32)).astype(bf16)

        over_rows(rows // step, step, add)
        hop_two(j).start()

    def stage_three(j):
        hop_one(j, 0).wait_recv()
        hop_two(j).wait_recv()
        for k in range(3):
            state(j, k).wait()
        slot = lax.rem(j, 3)

        def add(r):
            total = own[j, g, r, :].astype(f32) + recv1[j, g, r, :].astype(f32)
            total = total + recv2[j, 0, r, :].astype(f32) + recv3[j, r, :].astype(f32)
            own[j, g, r, :] = total.astype(bf16)
            new = adam_step(
                total.astype(bf16).astype(f32) / n_spot,
                adam[slot, 0, r, :], adam[slot, 1, r, :], adam[slot, 2, r, :],
            )[0]
            wg[j, r, cols(g * WIDE)] = new.astype(bf16)

        over_rows(rows // 64, 64, add)
        spread(j, 0).start()
        spread(j, 1).start()
        share(j).start()
        keep(j).start()

    def stage_four(j):
        spread(j, 0).wait_recv()
        spread(j, 2).start()

    def attend(i):
        @pl.when(i == 0)
        def _():
            q_copy.wait()
            k_copy.wait()
            v_copy.wait()
            k_send.wait_recv()
            v_send.wait_recv()

        span = tok + q_rows
        window = pl.ds(pl.multiple_of(i * q_rows, q_rows), span)
        q_at = pl.ds(pl.multiple_of(i * q_rows, q_rows), q_rows)
        out_at = pl.ds(pl.multiple_of(s * tok + i * q_rows, q_rows), q_rows)
        k_seg = segk[:, window]
        q_row = segk[:, pl.ds(pl.multiple_of(tok + i * q_rows, q_rows), q_rows)]
        q_seg = jnp.broadcast_to(q_row, (q_rows, q_rows)).T[:, :1]
        r_id = lax.broadcasted_iota(jnp.int32, (q_rows, span), 0)
        c_id = lax.broadcasted_iota(jnp.int32, (q_rows, span), 1)
        visible = (
            (c_id - tok <= r_id)
            & ((spot - 1) * tok + i * q_rows + c_id >= 0)
            & (k_seg == q_seg)
        )
        bias = jnp.where(visible, 0.0, -1e30)
        k_all = kbuf[window, :]
        v_all = vbuf[window, :]

        @pl.loop(0, queries.shape[1] // HD)
        def _(h):
            head = cols(h * HD)
            scores = lax.dot_general(
                qbuf[q_at, head], k_all, (((1,), (1,)), ((), ())), preferred_element_type=f32
            )
            scores = scores * (1.0 / HD**0.5) + bias
            expo = jnp.exp(scores - jnp.max(scores, axis=1, keepdims=True))
            probs = (expo * (1.0 / jnp.sum(expo, axis=1, keepdims=True))).astype(bf16)
            out = jnp.dot(probs, v_all, preferred_element_type=f32)
            attn[out_at, head] = out.astype(bf16)

        attn_part(i).start()

    def stage_five(j):
        @pl.when(j == 0)
        def _():
            for i in range(q_blocks):
                attn_part(i).wait_recv()

        spread(j, 1).wait_recv()
        spread(j, 2).wait_recv()

        def mul(r):
            out = jnp.dot(attn[r, :], wg[j], preferred_element_type=f32).astype(bf16)
            for b in range(4):
                recv1[j, b, r, :] = out[:, b * WIDE : (b + 1) * WIDE]

        over_rows(2 * tok // 256, 256, mul)
        ring(j, 0, 0).start()
        ring(j, 1, 0).start()

    def stage_ring(j, r):
        for d in range(2):
            ring(j, d, r - 1).wait_recv()
            b = lax.rem(t + 2 * n_tp - 1 - r, n_tp) if d == 0 else lax.rem(t + 1 + r, n_tp)

            def add(at):
                here = pl.ds(pl.multiple_of(d * tok + at.start, step), step)
                total = recv1[j, b, here, :].astype(f32) + rz[j, d, r - 1, at, :].astype(f32)
                recv1[j, b, here, :] = total.astype(bf16)

            over_rows(tok // step, step, add)
            if r < 3:
                ring(j, d, r).start()
        if r == 3:
            final_peer(j).start()
            final_own(j).start()

    def when(i, lag, fn):
        @pl.when((i >= lag) & (i < chunks + lag))
        def _():
            fn(i - lag)

    @pl.loop(0, chunks + 8)
    def _(i):
        @pl.when(i + 3 < chunks)
        def _():
            fetch(i + 3)

        @pl.when(i < chunks)
        def _():
            for k in range(3):
                state(i, k).start()
            stage_one(i)

        when(i, 1, stage_two)
        when(i, 2, stage_three)
        when(i, 3, stage_four)

        @pl.when(i < q_blocks)
        def _():
            attend(i)

        when(i, 4, stage_five)
        when(i, 5, lambda j: stage_ring(j, 1))
        when(i, 6, lambda j: stage_ring(j, 2))
        when(i, 7, lambda j: stage_ring(j, 3))

    k_send.wait_send()
    v_send.wait_send()

    @pl.loop(0, q_blocks)
    def _(i):
        attn_part(i).wait_send()

    @pl.loop(0, chunks)
    def _(j):
        for b in range(4):
            pair(j, b).wait_send()
        for k in range(2):
            hop_one(j, k).wait_send()
        hop_two(j).wait_send()
        share(j).wait()
        keep(j).wait()
        for k in range(3):
            spread(j, k).wait_send()
        for d in range(2):
            for r in range(3):
                ring(j, d, r).wait_send()
        final_peer(j).wait()
        final_own(j).wait()


def adam_step(gradient, master, moment, second):
    moment_new = beta_one * moment + (1.0 - beta_one) * gradient
    second_new = beta_two * second + (1.0 - beta_two) * gradient * gradient
    first_hat = moment_new / (1.0 - beta_one**10)
    second_hat = second_new / (1.0 - beta_two**10)
    master_new = master - learn_rate * (
        first_hat / (jnp.sqrt(second_hat) + adam_eps) + decay_rate * master
    )
    return master_new, moment_new, second_new


def fused_body(grads, master, moment, second, queries, keys, values, resid, segs):
    rows, blk = master.shape
    tok = queries.shape[0]
    half = blk // 2
    chunks = half // WIDE
    n_grp = lax.axis_size("grp")
    bf16 = jnp.bfloat16
    dma = pltpu.SemaphoreType.DMA
    anywhere = pl.BlockSpec(memory_space=pl.ANY)
    gsum, mixed = pl.pallas_call(
        fused_kernel,
        out_shape=(
            jax.ShapeDtypeStruct((rows, blk), bf16),
            jax.ShapeDtypeStruct(resid.shape, bf16),
        ),
        in_specs=[anywhere] * 7 + [pl.BlockSpec(memory_space=pltpu.VMEM)],
        out_specs=(anywhere, anywhere),
        scratch_shapes=[
            pltpu.VMEM((chunks, n_grp, rows, WIDE), bf16),
            pltpu.VMEM((chunks, n_grp, rows, WIDE), bf16),
            pltpu.VMEM((chunks, 2, rows, WIDE), bf16),
            pltpu.VMEM((chunks, rows, WIDE), bf16),
            pltpu.VMEM((chunks, rows, n_grp * WIDE), bf16),
            pltpu.VMEM((chunks, 2, 3, tok, WIDE), bf16),
            pltpu.VMEM((2 * tok, queries.shape[1]), bf16),
            pltpu.VMEM(queries.shape, bf16),
            pltpu.VMEM((2 * tok, HD), bf16),
            pltpu.VMEM((2 * tok, HD), bf16),
            pltpu.VMEM((3, 3, rows, WIDE), jnp.float32),
            pltpu.VMEM((1, 2 * tok), jnp.float32),
            dma((chunks, 4)), dma((chunks, 4)), dma((chunks, 4)),
            dma((chunks, 2)), dma((chunks, 2)),
            dma((chunks,)), dma((chunks,)),
            dma((chunks,)), dma((chunks,)), dma((chunks,)),
            dma((chunks, 3)), dma((chunks, 3)),
            dma((chunks, 6)), dma((chunks, 6)),
            dma((chunks,)), dma((chunks,)), dma((chunks,)),
            dma((3, 3)), dma((3,)), dma((2,)), dma((2,)),
            dma((tok // 128,)), dma((tok // 128,)),
        ],
        compiler_params=pltpu.CompilerParams(
            collective_id=0, has_side_effects=True, vmem_limit_bytes=62 * 1024 * 1024
        ),
        name="step",
    )(grads, master, moment, second, queries, keys, values, segs.reshape(1, -1))
    gradient = gsum.astype(jnp.float32) / (n_grp * lax.axis_size("seq"))
    master_new, moment_new, second_new = adam_step(gradient, master, moment, second)
    layer_out = (resid.astype(jnp.float32) + mixed.astype(jnp.float32)).astype(bf16)
    return (master_new, moment_new, second_new, layer_out)


def solution(mesh):
    placed = (
        P(("grp", "seq"), "tp", None),
        P("tp", "grp"),
        P("tp", "grp"),
        P("tp", "grp"),
        P(("grp", "seq"), "tp"),
        P(("grp", "seq"), None),
        P(("grp", "seq"), None),
        P(("grp", "seq"), "tp"),
        P(),
    )
    sizes = dict(mesh.shape)
    square = sizes["grp"] == 4 and sizes["tp"] == 4 and sizes["seq"] == 2
    return jax.shard_map(
        fused_body if square else body,
        mesh=mesh,
        in_specs=placed,
        out_specs=(P("tp", "grp"), P("tp", "grp"), P("tp", "grp"), P(("grp", "seq"), "tp")),
        check_vma=False,
    )
```
